32 devices in a mesh: dp: 16 (over z, x, core), feature: 2 (over y).
Axes of the slice: x: 2, y: 2, z: 4, core: 2. Of those that a mesh axis runs over, the one named last changes fastest.
Arguments:
- tokens: bfloat16 [4096, 16384], P('dp', 'feature'), may hold values from -6 to 6
- cotangent: bfloat16 [4096, 16384], P('dp', 'feature'), may hold values from -6 to 6
- first_factor: bfloat16 [128, 128, 512], P('dp', 'feature'), may hold values from -0.5 to 0.5
- second_factor: bfloat16 [512, 128, 128], P('dp', 'feature'), may hold values from -0.25 to 0.25
Outputs:
- output: bfloat16 [4096, 16384], P('dp', 'feature')
- grad_input: bfloat16 [4096, 16384], P('dp', 'feature')
- grad_first: float32 [128, 128, 512], P('dp', 'feature')
- grad_second: float32 [512, 128, 128], P('dp', 'feature')
The draws below stay inside these ranges and needn't reach their ends.
All inputs are finite; a program needn't handle non-finite values.
Results may differ from the reference program's by a relative error of at most 0.0058.
Values may be sent and summed in bfloat16 or wider, within the bound.
No kernel may reach another device: no remote copies, remote signals or barrier semaphores. Data moves between devices by JAX's collectives and lax.ppermute only.
A program may use at most 320 MiB of HBM per device.

```python
import jax
import jax.numpy as jnp
from jax import lax

D = 16384
NB = 128
TOK_DEV = 256
BI = 128
BH = 512
GROUP = 4
TOKENS = 4096


def block_scale(stream_key, shape, shards, least, largest):
    def one(position, shards_of):
        draws = jax.random.uniform(jax.random.fold_in(jax.random.fold_in(stream_key, 6), position), (shards_of,), jnp.float32, least / len(shards), largest / len(shards))
        return jnp.repeat(jnp.exp(draws), shape[position] // shards_of).reshape((-1,) + (1,) * (len(shape) - position - 1))

    loudness = one(*shards[0])
    for cut in shards[1:]:
        loudness = loudness * one(*cut)
    return loudness


def scatter_about(stream_key, shape, width, bound, split=(), kind=jnp.bfloat16):
    factor_of = block_scale(stream_key, shape, split, -0.22, 0.18) if split else 1.0
    result = jax.random.normal(stream_key, shape, jnp.float32) * width * factor_of
    return jnp.minimum(jnp.maximum(result, -bound), bound).astype(kind)


def setup_inputs(seed: int = 0) -> dict:
    key_of = jax.random.split(jax.random.key(seed), 5)
    return {
        "tokens": scatter_about(key_of[0], (TOKENS, D), 1.0, 6.0, ((0, 16), (1, 2))),
        "cotangent": scatter_about(key_of[1], (TOKENS, D), 1.0, 6.0, ((0, 16), (1, 2))),
        "first_factor": scatter_about(key_of[2], (BI, NB, BH), BI ** -0.5, 0.5, ((0, 16), (1, 2))),
        "second_factor": scatter_about(key_of[3], (BH, NB, BI), BH ** -0.5, 0.25, ((0, 16), (1, 2))),
    }


def gelu_exact(values):
    return jax.nn.gelu(values, approximate=False)

def permute_blocks(values):
    rows = values.shape[0]
    return values.reshape(rows, NB, NB, GROUP).transpose(0, 2, 1, 3).reshape(rows, NB, BH)

def reference(tokens, cotangent, first_factor, second_factor):
    w_first = first_factor.astype(jnp.float32)
    w_second = second_factor.astype(jnp.float32)
    block_count = TOKENS // TOK_DEV

    def one_block(totals, block_index):
        sum_first, sum_second = totals
        offset = (block_index * TOK_DEV).astype(jnp.int32)
        inputs = lax.dynamic_slice_in_dim(tokens, offset, TOK_DEV, 0).reshape(TOK_DEV, NB, BI).astype(jnp.float32)
        grads_out = lax.dynamic_slice_in_dim(cotangent, offset, TOK_DEV, 0).reshape(TOK_DEV, NB, BI).astype(jnp.float32)
        preact = jnp.einsum('tbi,ibj->tbj', inputs, w_first)
        activated, gelu_back = jax.vjp(gelu_exact, preact)
        activated = activated.astype(jnp.bfloat16)
        mixed_in = permute_blocks(activated).astype(jnp.float32)
        output = jnp.einsum('tck,kco->tco', mixed_in, w_second).astype(jnp.bfloat16)
        grad_mixed = jnp.einsum('tco,kco->tck', grads_out, w_second).astype(jnp.bfloat16)
        sum_second = sum_second + jnp.einsum('tck,tco->kco', mixed_in, grads_out)
        grad_act = permute_blocks(grad_mixed).astype(jnp.float32)
        grad_pre = gelu_back(grad_act)[0].astype(jnp.bfloat16).astype(jnp.float32)
        grad_input = jnp.einsum('tbj,ibj->tbi', grad_pre, w_first).astype(jnp.bfloat16)
        sum_first = sum_first + jnp.einsum('tbi,tbj->ibj', inputs, grad_pre)
        return ((sum_first, sum_second), (output.reshape(TOK_DEV, D), grad_input.reshape(TOK_DEV, D)))
    start_totals = (jnp.zeros((BI, NB, BH), jnp.float32), jnp.zeros((BH, NB, BI), jnp.float32))
    totals, stacked = lax.scan(one_block, start_totals, jnp.arange(block_count, dtype=jnp.int32))
    output = stacked[0].reshape(TOKENS, D)
    grad_input = stacked[1].reshape(TOKENS, D)
    return (output, grad_input, totals[0], totals[1])
```

```python
import jax
import jax.numpy as jnp
from jax import lax
from jax.sharding import PartitionSpec as P


def gelu_exact(values):
    return jax.nn.gelu(values, approximate=False)


def exchange(pieces_for, place):
    count = lax.axis_size("feature")
    here = lax.axis_index("feature")
    for step in range(count):
        target = (here + step) % count
        source = (here - step) % count
        piece = pieces_for(target)
        if step:
            piece = lax.ppermute(piece, "feature", [(i, (i + step) % count) for i in range(count)])
        place(source, piece)


def all_parts(values, axis):
    count = lax.axis_size("feature")
    size = values.shape[axis]
    whole = [jnp.zeros(values.shape[:axis] + (size * count,) + values.shape[axis + 1 :], values.dtype)]

    def place(source, piece):
        whole[0] = lax.dynamic_update_slice_in_dim(whole[0], piece, source * size, axis)

    exchange(lambda target: values, place)
    return whole[0]


def swap_parts(values, split_axis, concat_axis):
    count = lax.axis_size("feature")
    size = values.shape[split_axis] // count
    width = values.shape[concat_axis]
    shape = list(values.shape)
    shape[split_axis] = size
    shape[concat_axis] = width * count
    whole = [jnp.zeros(shape, values.dtype)]

    def place(source, piece):
        whole[0] = lax.dynamic_update_slice_in_dim(whole[0], piece, source * width, concat_axis)

    exchange(lambda target: lax.dynamic_slice_in_dim(values, target * size, size, split_axis), place)
    return whole[0]


def sum_parts(values, axis):
    count = lax.axis_size("feature")
    size = values.shape[axis] // count
    total = [0.0]

    def place(source, piece):
        total[0] = total[0] + piece.astype(jnp.float32)

    here = lax.axis_index("feature")
    for step in range(count):
        target = (here + step) % count
        piece = lax.dynamic_slice_in_dim(values, target * size, size, axis)
        if step:
            piece = lax.ppermute(
                piece.astype(jnp.bfloat16), "feature", [(i, (i + step) % count) for i in range(count)]
            )
        place(None, piece)
    return total[0]


def scatter_rows(values):
    summed = lax.psum_scatter(values.astype(jnp.bfloat16), "dp", scatter_dimension=0, tiled=True)
    return summed


def per_device(tokens, cotangent, first_factor, second_factor):
    count = lax.axis_size("feature")
    local_blocks = first_factor.shape[1]
    all_blocks = local_blocks * count
    hidden_block = first_factor.shape[2]
    in_block = second_factor.shape[2]
    group = hidden_block // all_blocks
    rows = tokens.shape[0]
    bf16 = jnp.bfloat16
    f32 = jnp.float32
    first_mine = swap_parts(first_factor, 2, 1)
    inputs = all_parts(tokens, 1).reshape(rows, all_blocks, in_block)
    grads_out = cotangent.reshape(rows, local_blocks, in_block)
    first_whole = lax.all_gather(first_mine, "dp", axis=0, tiled=True)
    second_whole = lax.all_gather(second_factor, "dp", axis=0, tiled=True)
    preact = jnp.einsum("tbi,ibj->bjt", inputs, first_whole, preferred_element_type=f32)
    activated, gelu_back = jax.vjp(gelu_exact, preact)
    mixed_in = (
        activated.astype(bf16)
        .reshape(all_blocks, local_blocks, group, rows)
        .transpose(1, 0, 2, 3)
        .reshape(local_blocks, hidden_block, rows)
    )
    output = jnp.einsum("ckt,kco->tco", mixed_in, second_whole, preferred_element_type=f32)
    output = output.astype(bf16).reshape(rows, local_blocks * in_block)
    grad_second = jnp.einsum("ckt,tco->kco", mixed_in, grads_out, preferred_element_type=f32)
    grad_second = scatter_rows(grad_second).astype(f32)
    grad_mixed = jnp.einsum("tco,kco->ckt", grads_out, second_whole, preferred_element_type=f32)
    grad_act = (
        grad_mixed.astype(bf16)
        .reshape(local_blocks, all_blocks, group, rows)
        .transpose(1, 0, 2, 3)
        .reshape(all_blocks, local_blocks * group, rows)
    )
    grad_pre = gelu_back(grad_act.astype(f32))[0].astype(bf16)
    grad_first = jnp.einsum("tbi,bjt->ibj", inputs, grad_pre, preferred_element_type=f32)
    grad_input = jnp.einsum("bjt,ibj->tbi", grad_pre, first_whole, preferred_element_type=f32)
    grad_input = sum_parts(grad_input.reshape(rows, all_blocks * in_block), 1).astype(bf16)
    grad_first = swap_parts(scatter_rows(grad_first), 1, 2).astype(f32)
    return (output, grad_input, grad_first, grad_second)


def solution(mesh):
    placed = (
        P("dp", "feature"),
        P("dp", "feature"),
        P("dp", "feature", None),
        P("dp", "feature", None),
    )
    return jax.shard_map(
        per_device, mesh=mesh, in_specs=placed, out_specs=placed, check_vma=False
    )
```

```python
import functools
import math

import jax
import jax.numpy as jnp
from jax import lax
from jax.experimental import pallas as pl
from jax.experimental.pallas import tpu as pltpu
from jax.sharding import PartitionSpec as P

BF16 = jnp.bfloat16
F32 = jnp.float32
SUBLANES = 8
VMEM = 60 * 1024 * 1024


def contract(left, right, dims):
    return lax.dot_general(left, right, ((dims[:1], dims[1:]), ((), ())), preferred_element_type=F32)


def regroup(parts, group):
    count = len(parts)
    if count == 1:
        return parts
    row = lax.broadcasted_iota(jnp.int32, parts[0].shape, 1)
    results = []
    for r in range(count):
        total = None
        for p in range(count):
            shift = (p - r) * group % SUBLANES
            piece = pltpu.roll(parts[p], shift, 1) if shift else parts[p]
            total = piece if total is None else jnp.where(row < p * group, total, piece)
        results.append(total)
    return results


def back_kernel(second_ref, grads_ref, mixed_ref):
    blocks, _, width = second_ref.shape
    for c in range(blocks):
        grads = grads_ref[:, c * width : (c + 1) * width]
        mixed_ref[c] = contract(second_ref[c], grads, (1, 1)).astype(BF16)


def middle_kernel(group, where_ref, first_ref, inputs_ref, mixed_ref, hidden_ref, grad_in_ref, grad_first_ref):
    blocks, _, width = first_ref.shape
    rows = inputs_ref.shape[-1]
    lots = SUBLANES // group
    tile = 2 * lots
    half_root = math.sqrt(0.5)
    for low in range(0, blocks, tile):
        outs = []
        first_row = low * group
        grads = []
        for half in range(2):
            start = first_row + half * SUBLANES
            grads += regroup(
                [
                    mixed_ref[:, r, start : start + SUBLANES, :].astype(F32)
                    for r in range(lots)
                ],
                group,
            )
        for k in range(tile):
            b = low + k
            first = first_ref[b]
            inputs = inputs_ref[b]
            pre = contract(first, inputs, (0, 0))
            rise = 0.5 + 0.5 * lax.erf(pre * half_root)
            slope = rise + pre * (jnp.exp(-0.5 * pre * pre) * (half_root / math.sqrt(math.pi)))
            outs.append((pre * rise).reshape(width // SUBLANES, SUBLANES, rows))
            grad = (grads[k].reshape(width, rows) * slope).astype(BF16)
            grad_in_ref[b] = contract(first, grad, (1, 0)).astype(BF16)
            grad_first_ref[b] = contract(inputs, grad, (1, 1)).astype(BF16)
        front = regroup(outs[:lots], group)
        behind = regroup(outs[lots:], group)
        for r in range(lots):
            both = jnp.concatenate([front[r], behind[r]], axis=1).astype(BF16)
            hidden_ref[:, r, first_row : first_row + 2 * SUBLANES, :] = both


def front_kernel(second_ref, grads_ref, hidden_ref, out_ref, grad_second_ref):
    blocks, _, width = second_ref.shape
    for c in range(blocks):
        grads = grads_ref[:, c * width : (c + 1) * width]
        hidden = hidden_ref[c]
        out_ref[c] = contract(second_ref[c], hidden, (0, 0)).astype(BF16)
        grad_second_ref[c] = contract(hidden, grads, (1, 0)).astype(BF16)


def params():
    return pltpu.CompilerParams(vmem_limit_bytes=VMEM)


def cost(flops, size, special=0):
    return pl.CostEstimate(flops=flops, bytes_accessed=size, transcendentals=special)


def per_device(tokens, cotangent, first_factor, second_factor):
    count = lax.axis_size("feature")
    here = lax.axis_index("feature")
    own = first_factor.shape[1]
    blocks = own * count
    hidden = first_factor.shape[2]
    part = hidden // count
    width = second_factor.shape[2]
    group = hidden // blocks
    rows = tokens.shape[0]
    lots = SUBLANES // group

    def send(values, step):
        if step % count == 0:
            return values
        return lax.ppermute(values, "feature", [(i, (i + step) % count) for i in range(count)])

    first_shard = first_factor.transpose(1, 0, 2)
    second_shard = second_factor.transpose(1, 0, 2)
    second_whole = lax.all_gather(second_shard, "dp", axis=1, tiled=True)
    turned = tokens.T
    first_parts = []
    input_parts = []
    for step in range(count):
        to = (here + step) % count
        piece = send(lax.dynamic_slice_in_dim(first_shard, to * part, part, 2), step)
        first_parts.append(lax.all_gather(piece, "dp", axis=1, tiled=True))
        input_parts.append(send(turned, step).reshape(own, width, rows))

    per_c = 4 if own % 4 == 0 else 1
    steps_c = own // per_c
    second_spec = pl.BlockSpec((per_c, hidden, width), lambda i: (i, 0, 0))
    grads_spec = pl.BlockSpec((rows, per_c * width), lambda i: (0, i))
    hidden_spec = pl.BlockSpec((per_c, hidden, rows), lambda i: (i, 0, 0))
    work = 2 * rows * own * hidden * width
    mixed = pl.pallas_call(
        back_kernel,
        grid=(steps_c,),
        in_specs=[second_spec, grads_spec],
        out_specs=hidden_spec,
        out_shape=jax.ShapeDtypeStruct((own, hidden, rows), BF16),
        compiler_params=params(),
        cost_estimate=cost(work, 2 * own * (hidden * width + rows * width + hidden * rows)),
        name="back",
    )(second_whole, cotangent)
    mixed = mixed.reshape(own // lots, lots, hidden, rows)

    per_b = 2 * lots
    steps_b = own // per_b
    activated = None
    grad_inputs = []
    grad_firsts = []
    for step in range(count):
        source = (here - step) % count
        where = (source * steps_b).astype(jnp.int32).reshape(1)
        block_rows = per_b * group
        first_spec = pl.BlockSpec((per_b, width, part), lambda i, w: (i, 0, 0))
        token_spec = pl.BlockSpec((per_b, width, rows), lambda i, w: (i, 0, 0))
        mix_spec = pl.BlockSpec((own // lots, lots, block_rows, rows), lambda i, w: (0, 0, w[0] + i, 0))
        operands = [where, first_parts[step], input_parts[step], mixed]
        in_specs = [first_spec, token_spec, mix_spec]
        body = functools.partial(middle_kernel, group)
        aliases = {}
        if activated is not None:
            operands.append(activated)
            in_specs.append(pl.BlockSpec(memory_space=pl.ANY))
            aliases = {4: 0}
            body = functools.partial(skip_operand, body)
        activated, grad_in, grad_first = pl.pallas_call(
            body,
            grid_spec=pltpu.PrefetchScalarGridSpec(
                num_scalar_prefetch=1,
                grid=(steps_b,),
                in_specs=in_specs,
                out_specs=[mix_spec, token_spec, first_spec],
            ),
            out_shape=[
                jax.ShapeDtypeStruct(mixed.shape, BF16),
                jax.ShapeDtypeStruct((own, width, rows), BF16),
                jax.ShapeDtypeStruct((own, width, part), BF16),
            ],
            input_output_aliases=aliases,
            compiler_params=params(),
            cost_estimate=cost(
                3 * work // count,
                4 * own * (width * part + width * rows + part * rows),
                2 * own * part * rows,
            ),
            name="middle",
        )(*operands)
        grad_inputs.append(send(grad_in, -step))
        scattered = lax.psum_scatter(grad_first, "dp", scatter_dimension=1, tiled=True)
        grad_firsts.append(send(scattered, -step))
    activated = activated.reshape(own, hidden, rows)

    output, grad_second = pl.pallas_call(
        front_kernel,
        grid=(steps_c,),
        in_specs=[second_spec, grads_spec, hidden_spec],
        out_specs=[pl.BlockSpec((per_c, width, rows), lambda i: (i, 0, 0)), second_spec],
        out_shape=[
            jax.ShapeDtypeStruct((own, width, rows), BF16),
            jax.ShapeDtypeStruct((own, hidden, width), BF16),
        ],
        compiler_params=params(),
        cost_estimate=cost(2 * work, 2 * own * (2 * hidden * width + 2 * rows * width + hidden * rows)),
        name="front",
    )(second_whole, cotangent, activated)
    grad_second = lax.psum_scatter(grad_second, "dp", scatter_dimension=1, tiled=True)
    grad_second = grad_second.transpose(1, 0, 2).astype(F32)
    output = output.reshape(own * width, rows).T

    total = functools.reduce(jnp.add, [piece.astype(F32) for piece in grad_inputs])
    grad_input = total.reshape(own * width, rows).T.astype(BF16)

    shape = (first_factor.shape[1], first_factor.shape[0], hidden)
    grad_first = jnp.zeros(shape, F32)
    for step in range(count):
        owner = (here + step) % count
        grad_first = lax.dynamic_update_slice_in_dim(
            grad_first, grad_firsts[step].astype(F32), owner * part, 2
        )
    return (output, grad_input, grad_first.transpose(1, 0, 2), grad_second)


def skip_operand(body, *refs):
    body(*refs[:4], *refs[5:])


def solution(mesh):
    placed = (
        P("dp", "feature"),
        P("dp", "feature"),
        P("dp", "feature", None),
        P("dp", "feature", None),
    )
    return jax.shard_map(
        per_device, mesh=mesh, in_specs=placed, out_specs=placed, check_vma=False
    )
```

```python
import functools
import math

import jax
import jax.numpy as jnp
import numpy as np
from jax import lax
from jax.experimental import pallas as pl
from jax.experimental.pallas import tpu as pltpu
from jax.sharding import PartitionSpec as P

BF16 = jnp.bfloat16
F32 = jnp.float32
SUBLANES = 8
VMEM = 60 * 1024 * 1024


def contract(left, right, dims):
    return lax.dot_general(left, right, ((dims[:1], dims[1:]), ((), ())), preferred_element_type=F32)


def regroup(parts, group):
    count = len(parts)
    if count == 1:
        return parts
    row = lax.broadcasted_iota(jnp.int32, parts[0].shape, 1)
    results = []
    for r in range(count):
        total = None
        for p in range(count):
            shift = (p - r) * group % SUBLANES
            piece = pltpu.roll(parts[p], shift, 1) if shift else parts[p]
            total = piece if total is None else jnp.where(row < p * group, total, piece)
        results.append(total)
    return results


def gathered(mine, other, core):
    chips, rows, lanes = mine.shape
    first = core == 0
    low = jnp.where(first, mine, other)
    high = jnp.where(first, other, mine)
    return jnp.concatenate([low, high], axis=1).reshape(2 * chips * rows, lanes)


def back_kernel(core_ref, mine_ref, other_ref, grads_ref, mixed_ref):
    blocks = mine_ref.shape[0]
    width = mine_ref.shape[-1]
    for c in range(blocks):
        grads = grads_ref[:, c * width : (c + 1) * width]
        second = gathered(mine_ref[c], other_ref[c], core_ref[0])
        mixed_ref[c] = contract(second, grads, (1, 1)).astype(BF16)


def middle_kernel(
    group, where_ref, core_ref, mine_ref, other_ref, inputs_ref, mixed_ref, hidden_ref, grad_in_ref, grad_first_ref
):
    blocks = mine_ref.shape[0]
    width = mine_ref.shape[-1]
    rows = inputs_ref.shape[-1]
    lots = SUBLANES // group
    tile = 2 * lots
    half_root = math.sqrt(0.5)
    for low in range(0, blocks, tile):
        outs = []
        first_row = low * group
        grads = []
        for half in range(2):
            start = first_row + half * SUBLANES
            grads += regroup(
                [mixed_ref[:, r, start : start + SUBLANES, :].astype(F32) for r in range(lots)], group
            )
        for k in range(tile):
            b = low + k
            first = gathered(mine_ref[b].astype(F32), other_ref[b].astype(F32), core_ref[0]).astype(BF16)
            inputs = inputs_ref[b]
            pre = contract(first, inputs, (0, 0))
            rise = 0.5 + 0.5 * lax.erf(pre * half_root)
            slope = rise + pre * (jnp.exp(-0.5 * pre * pre) * (half_root / math.sqrt(math.pi)))
            outs.append((pre * rise).reshape(width // SUBLANES, SUBLANES, rows))
            grad = (grads[k].reshape(width, rows) * slope).astype(BF16)
            grad_in_ref[b] = contract(first, grad, (1, 0)).astype(BF16)
            grad_first_ref[b] = contract(inputs, grad, (1, 1)).astype(BF16)
        front = regroup(outs[:lots], group)
        behind = regroup(outs[lots:], group)
        for r in range(lots):
            both = jnp.concatenate([front[r], behind[r]], axis=1).astype(BF16)
            hidden_ref[:, r, first_row : first_row + 2 * SUBLANES, :] = both


def front_kernel(core_ref, mine_ref, other_ref, grads_ref, hidden_ref, out_ref, grad_second_ref):
    blocks = mine_ref.shape[0]
    width = mine_ref.shape[-1]
    for c in range(blocks):
        grads = grads_ref[:, c * width : (c + 1) * width]
        second = gathered(mine_ref[c], other_ref[c], core_ref[0])
        hidden = hidden_ref[c]
        out_ref[c] = contract(second, hidden, (0, 0)).astype(BF16)
        grad_second_ref[c] = contract(hidden, grads, (1, 0)).astype(BF16)


def skip_operand(body, at, *refs):
    body(*refs[:at], *refs[at + 1 :])


def params():
    return pltpu.CompilerParams(vmem_limit_bytes=VMEM)


def cost(flops, size, special=0):
    return pl.CostEstimate(flops=flops, bytes_accessed=size, transcendentals=special)


def ring_order(mesh):
    axis = mesh.axis_names.index("dp")
    line = np.moveaxis(mesh.devices, axis, 0).reshape(mesh.shape["dp"], -1)[:, 0]
    chips = len(line) // 2
    places = [getattr(line[2 * q], "coords", None) for q in range(chips)]
    inner = chips
    if places[0] is not None:
        inner = 1
        varies = lambda q: [k for k in range(3) if places[q][k] != places[0][k]]
        while inner < chips and len(varies(inner)) == 1 and varies(inner) == varies(1):
            inner += 1
    if chips % inner:
        inner = chips
    outer = chips // inner
    grid = [[o * inner + k for k in range(inner)] for o in range(outer)]
    if inner == 2 and outer > 2:
        grid = [list(column) for column in zip(*grid)]
    order = []
    for k, row in enumerate(grid):
        order += row if k % 2 == 0 else row[::-1]
    return order


class Ring:
    def __init__(self, order):
        self.order = order
        self.chips = len(order)
        self.up = self.chips // 2
        self.down = (self.chips - 1) // 2
        position = [0] * self.chips
        for p, q in enumerate(order):
            position[q] = p
        index = lax.axis_index("dp")
        self.core = index % 2
        offsets = range(-self.up, self.up + 1)
        table = [[order[(position[q] + k) % self.chips] for k in offsets] for q in range(self.chips)]
        row = jnp.asarray(table, jnp.int32)[index // 2]
        self.chip = {k: row[k + self.up] for k in offsets}

    def move(self, values, step):
        n = self.chips
        pairs = [
            (2 * self.order[p] + core, 2 * self.order[(p + step) % n] + core) for p in range(n) for core in range(2)
        ]
        return lax.ppermute(values, "dp", pairs)

    def swap(self, values):
        return lax.ppermute(values, "dp", [(k, k ^ 1) for k in range(2 * self.chips)])

    def gather(self, shard):
        blocks, rows, lanes = shard.shape
        mine = jnp.zeros((blocks, self.chips, rows, lanes), shard.dtype)

        def put(mine, piece, k):
            return lax.dynamic_update_slice_in_dim(mine, piece[:, None], self.chip[k], 1)

        mine = put(mine, shard, 0)
        rising = falling = shard
        for k in range(1, self.up + 1):
            rising = self.move(rising, 1)
            mine = put(mine, rising, -k)
            if k <= self.down:
                falling = self.move(falling, -1)
                mine = put(mine, falling, k)
        return mine, self.swap(mine)

    def scatter(self, parts):
        blocks, _, lanes = parts.shape
        parts = parts.reshape(blocks, self.chips, 2, -1, lanes)
        rows = parts.shape[3]
        given = lax.dynamic_slice_in_dim(parts, 1 - self.core, 1, 2)[:, :, 0]
        got = self.swap(given)

        def own(k):
            at = self.chip[k]
            zero = jnp.zeros((), at.dtype)
            one = lax.dynamic_slice(parts, (zero, at, self.core, zero, zero), (blocks, 1, 1, rows, lanes))
            two = lax.dynamic_slice(got, (zero, at, zero, zero), (blocks, 1, rows, lanes))
            return one[:, 0, 0].astype(F32) + two[:, 0].astype(F32)

        rising = falling = None
        for k in range(self.up, 0, -1):
            total = own(k)
            if rising is not None:
                total = total + rising.astype(F32)
            rising = self.move(total.astype(BF16), 1)
            if k <= self.down:
                total = own(-k)
                if falling is not None:
                    total = total + falling.astype(F32)
                falling = self.move(total.astype(BF16), -1)
        total = own(0) + rising.astype(F32)
        if falling is not None:
            total = total + falling.astype(F32)
        return total


def per_device(order, tokens, cotangent, first_factor, second_factor):
    count = lax.axis_size("feature")
    here = lax.axis_index("feature")
    ring = Ring(order)
    chips = ring.chips
    own = first_factor.shape[1]
    blocks = own * count
    hidden = first_factor.shape[2]
    part = hidden // count
    width = second_factor.shape[2]
    group = hidden // blocks
    rows = tokens.shape[0]
    lots = SUBLANES // group
    core = ring.core.astype(jnp.int32).reshape(1)

    def send(values, step):
        if step % count == 0:
            return values
        return lax.ppermute(values, "feature", [(i, (i + step) % count) for i in range(count)])

    def many(values):
        return values[0] if len(values) == 1 else jnp.concatenate(values, axis=0)

    first_shard = first_factor.transpose(1, 0, 2)
    second_shard = second_factor.transpose(1, 0, 2)
    pieces = []
    for step in range(count):
        to = (here + step) % count
        pieces.append(send(lax.dynamic_slice_in_dim(first_shard, to * part, part, 2), step))
    turned = tokens.T
    lots_of_steps = [[0], list(range(1, count))] if count > 1 else [[0]]
    second_mine, second_other = ring.gather(second_shard)
    firsts = [ring.gather(many([pieces[s] for s in steps])) for steps in lots_of_steps]
    inputs = [many([send(turned, s).reshape(own, width, rows) for s in steps]) for steps in lots_of_steps]

    per_c = 4 if own % 4 == 0 else 1
    steps_c = own // per_c
    piece_rows = hidden // (2 * chips)
    half_spec = pl.BlockSpec((per_c, chips, piece_rows, width), lambda i, w: (i, 0, 0, 0))
    grads_spec = pl.BlockSpec((rows, per_c * width), lambda i, w: (0, i))
    hidden_spec = pl.BlockSpec((per_c, hidden, rows), lambda i, w: (i, 0, 0))
    work = 2 * rows * own * hidden * width
    mixed = pl.pallas_call(
        back_kernel,
        grid_spec=pltpu.PrefetchScalarGridSpec(
            num_scalar_prefetch=1,
            grid=(steps_c,),
            in_specs=[half_spec, half_spec, grads_spec],
            out_specs=hidden_spec,
        ),
        out_shape=jax.ShapeDtypeStruct((own, hidden, rows), BF16),
        compiler_params=params(),
        cost_estimate=cost(work, 2 * own * (hidden * width + rows * width + hidden * rows)),
        name="back",
    )(core, second_mine, second_other, cotangent)
    mixed = mixed.reshape(own // lots, lots, hidden, rows)

    per_b = 2 * lots
    steps_b = own // per_b
    activated = None
    grad_input = None
    grad_firsts = [None] * count
    for steps, (mine, other), tokens_in in zip(lots_of_steps, firsts, inputs):
        size = own * len(steps)
        sources = jnp.stack([(here - s) % count for s in steps]).astype(jnp.int32)
        where = (sources[:, None] * steps_b + jnp.arange(steps_b, dtype=jnp.int32)).reshape(-1)
        block_rows = per_b * group
        part_rows = width // (2 * chips)
        half_spec_b = pl.BlockSpec((per_b, chips, part_rows, part), lambda i, w, c: (i, 0, 0, 0))
        first_spec = pl.BlockSpec((per_b, width, part), lambda i, w, c: (i, 0, 0))
        token_spec = pl.BlockSpec((per_b, width, rows), lambda i, w, c: (i, 0, 0))
        mix_spec = pl.BlockSpec((own // lots, lots, block_rows, rows), lambda i, w, c: (0, 0, w[i], 0))
        operands = [where, core, mine, other, tokens_in, mixed]
        in_specs = [half_spec_b, half_spec_b, token_spec, mix_spec]
        body = functools.partial(middle_kernel, group)
        aliases = {}
        if activated is not None:
            operands.append(activated)
            in_specs.append(pl.BlockSpec(memory_space=pl.ANY))
            aliases = {6: 0}
            body = functools.partial(skip_operand, body, 6)
        activated, grad_in, grad_first = pl.pallas_call(
            body,
            grid_spec=pltpu.PrefetchScalarGridSpec(
                num_scalar_prefetch=2,
                grid=(size // per_b,),
                in_specs=in_specs,
                out_specs=[mix_spec, token_spec, first_spec],
            ),
            out_shape=[
                jax.ShapeDtypeStruct(mixed.shape, BF16),
                jax.ShapeDtypeStruct((size, width, rows), BF16),
                jax.ShapeDtypeStruct((size, width, part), BF16),
            ],
            input_output_aliases=aliases,
            compiler_params=params(),
            cost_estimate=cost(
                3 * work * len(steps) // count,
                4 * size * (width * part + width * rows + part * rows),
                2 * size * part * rows,
            ),
            name="middle",
        )(*operands)
        scattered = ring.scatter(grad_first)
        for k, s in enumerate(steps):
            came = send(grad_in[k * own : (k + 1) * own], -s).astype(F32)
            grad_input = came if grad_input is None else grad_input + came
            grad_firsts[s] = send(scattered[k * own : (k + 1) * own], -s)
    activated = activated.reshape(own, hidden, rows)

    output, grad_second = pl.pallas_call(
        front_kernel,
        grid_spec=pltpu.PrefetchScalarGridSpec(
            num_scalar_prefetch=1,
            grid=(steps_c,),
            in_specs=[half_spec, half_spec, grads_spec, hidden_spec],
            out_specs=[
                pl.BlockSpec((per_c, width, rows), lambda i, w: (i, 0, 0)),
                pl.BlockSpec((per_c, hidden, width), lambda i, w: (i, 0, 0)),
            ],
        ),
        out_shape=[
            jax.ShapeDtypeStruct((own, width, rows), BF16),
            jax.ShapeDtypeStruct((own, hidden, width), BF16),
        ],
        compiler_params=params(),
        cost_estimate=cost(2 * work, 2 * own * (2 * hidden * width + 2 * rows * width + hidden * rows)),
        name="front",
    )(core, second_mine, second_other, cotangent, activated)
    grad_second = ring.scatter(grad_second).transpose(1, 0, 2)
    output = output.reshape(own * width, rows).T
    grad_input = grad_input.reshape(own * width, rows).T.astype(BF16)

    shape = (first_factor.shape[1], first_factor.shape[0], hidden)
    grad_first = jnp.zeros(shape, F32)
    for step in range(count):
        owner = (here + step) % count
        grad_first = lax.dynamic_update_slice_in_dim(grad_first, grad_firsts[step], owner * part, 2)
    return (output, grad_input, grad_first.transpose(1, 0, 2), grad_second)


def solution(mesh):
    placed = (
        P("dp", "feature"),
        P("dp", "feature"),
        P("dp", "feature", None),
        P("dp", "feature", None),
    )
    return jax.shard_map(
        functools.partial(per_device, ring_order(mesh)),
        mesh=mesh,
        in_specs=placed,
        out_specs=placed,
        check_vma=False,
    )
```
